32 devices in a mesh: dp: 4 (over z), ctx: 4 (over y, x), tensor: 2 (over core).
Axes of the slice: x: 2, y: 2, z: 4, core: 2. Of those that a mesh axis runs over, the one named last changes fastest.
Arguments:
- tokens: bfloat16 [4096, 1024], P(('dp', 'ctx')), may hold values from -6 to 6
- doc_lengths: int32 [4, 8], P('dp'), may hold values from 1 to 512, 1024 in all within a row
- gain_attn: bfloat16 [1024], P('dp'), may hold values from 0.5 to 1.5
- w_qkv: bfloat16 [3, 1024, 1024], P(None, 'dp', 'tensor'), may hold values from -0.1875 to 0.1875
- w_attn_out: bfloat16 [1024, 1024], P('tensor', 'dp'), may hold values from -0.5 to 0.5
- gain_mlp: bfloat16 [1024], P('dp'), may hold values from 0.5 to 1.5
- w_in: bfloat16 [2, 1024, 2624], P(None, 'dp', 'tensor'), may hold values from -0.1875 to 0.1875
- w_mlp_out: bfloat16 [2624, 1024], P('tensor', 'dp'), may hold values from -0.125 to 0.125
- cotangent: bfloat16 [4096, 1024], P(('dp', 'ctx')), may hold values from -6 to 6
Outputs:
- out_tokens: bfloat16 [4096, 1024], P(('dp', 'ctx'))
- grad_tokens: float32 [4096, 1024], P(('dp', 'ctx'))
- grad_gain_attn: float32 [1024], P('dp')
- grad_w_qkv: float32 [3, 1024, 1024], P(None, 'dp', 'tensor')
- grad_w_attn_out: float32 [1024, 1024], P('tensor', 'dp')
- grad_gain_mlp: float32 [1024], P('dp')
- grad_w_in: float32 [2, 1024, 2624], P(None, 'dp', 'tensor')
- grad_w_mlp_out: float32 [2624, 1024], P('tensor', 'dp')
The draws below stay inside these ranges and needn't reach their ends.
Inputs may be any that keep to these rules, and one draw needn't show every extreme that they name: `doc_lengths`: each row sums to 1024, and the longest document of each row has exactly half of 1024 tokens.
All inputs are finite; a program needn't handle non-finite values.
Results may differ from the reference program's by a relative error of at most 0.013.
Values may be sent and summed in bfloat16 or wider, within the bound.
A program may use at most 128 MiB of HBM per device.

```python
import math
import jax
import jax.numpy as jnp
import numpy as np
from jax import lax

D = 1024
HD = 64
FF = 2624
DOCS = 8
TOK_DEV = 256
SPAN = 1024
SPANS = 4
TOKENS = 4096
N_CTX = 4


def draw_tokens(key, part):
    values = jnp.clip(jax.random.normal(jax.random.fold_in(key, 11), (TOKENS, D), jnp.float32), -6.0, 6.0)
    return values.astype(jnp.bfloat16)


def draw_w_qkv(key, part):
    spread = D ** (-0.5)
    values = jnp.clip(jax.random.normal(jax.random.fold_in(key, 21), (3, D, D), jnp.float32), -6.0, 6.0) * spread
    return values.astype(jnp.bfloat16)


def block_scale(key, extent, cuts, low, top_value):
    level = 1.0
    for dim, shards_of in cuts:
        draws = jax.random.uniform(jax.random.fold_in(jax.random.fold_in(key, 6), dim), (shards_of,), jnp.float32, low / len(cuts), top_value / len(cuts))
        level = level * jnp.repeat(jnp.exp(draws), extent[dim] // shards_of).reshape((-1,) + (1,) * (len(extent) - 1 - dim))
    return level


def split_up(count, total, most, lean):
    loads = [(1 << 20) // math.isqrt(grade ** lean) + 1 for grade in range(2, count + 1)]
    rest, counts = total - most - (count - 1), [1] * (count - 1)
    while rest > 0:
        candidates = [i for i in range(count - 1) if counts[i] < most]
        pool, left = sum([loads[i] for i in candidates]), rest
        for i in candidates:
            extra = min(most - counts[i], max(1, left * loads[i] // pool), rest)
            counts[i] = counts[i] + extra
            rest = rest - extra
    return np.array([most] + counts)


def uneven_parts(key, number_of, total, most, skew):
    if number_of == 2:
        one = jax.random.randint(key, (), max(1, total - most), min(most, total - 1) + 1)
        return jnp.stack([one, total - one])
    sizes = jnp.asarray(split_up(number_of, total, most, skew), jnp.int32)
    pairs = (number_of - 1) // 2
    source_of, sink = sizes[1:1 + 2 * pairs:2], sizes[2:2 + 2 * pairs:2]
    room = jnp.minimum(source_of - 1, most - sink)
    shifted = jax.random.randint(jax.random.fold_in(key, 1), (pairs,), 0, 1 << 20) % (room + 1)
    sizes = sizes.at[1:1 + 2 * pairs:2].set(source_of - shifted).at[2:2 + 2 * pairs:2].set(sink + shifted)
    return sizes[jax.random.permutation(jax.random.fold_in(key, 2), number_of)]


def centred(key, dims, scale, bound, cuts=(), kind=jnp.bfloat16):
    values = jax.random.normal(key, dims, jnp.float32) * scale
    if len(cuts) > 0:
        values = block_scale(key, dims, cuts, -0.22, 0.18) * values
    return jnp.clip(values, min=-bound, max=bound).astype(kind)


def setup_inputs(seed: int = 0) -> dict:
    splits = jax.random.split(jax.random.key(seed), 10)
    return {
        "tokens": draw_tokens(jax.random.fold_in(splits[9], 71), 0),
        "doc_lengths": jax.vmap(lambda own: uneven_parts(own, DOCS, SPAN, SPAN // 2, 2))(jax.random.split(splits[1], SPANS)).reshape((SPANS, DOCS)).astype(jnp.int32),
        "gain_attn": jnp.clip(1.0 + 0.1 * jax.random.normal(splits[2], (D,), jnp.float32), 0.5, 1.5).astype(jnp.bfloat16),
        "w_qkv": draw_w_qkv(jax.random.fold_in(splits[9], 71), 0),
        "w_attn_out": centred(splits[4], (D, D), (D // 8) ** -0.5, 0.5, ((0, 2), (1, 4))),
        "gain_mlp": jnp.clip(1.0 + 0.1 * jax.random.normal(splits[5], (D,), jnp.float32), 0.5, 1.5).astype(jnp.bfloat16),
        "w_in": centred(splits[6], (2, D, FF), D ** -0.5, 0.1875, ((1, 4), (2, 2))),
        "w_mlp_out": centred(splits[7], (FF, D), FF ** -0.5, 0.125, ((0, 2), (1, 4))),
        "cotangent": centred(splits[8], (TOKENS, D), 1.0, 6.0, ((0, 16),)),
    }


NORM_EPS = 1e-05
ROPE_BASE = 160000.0
MASK_FILL = -1e+30
INV_ROOT_TWO = 1.0 / math.sqrt(2.0)
INV_ROOT_TWO_PI = 1.0 / math.sqrt(2.0 * math.pi)

def norm_forward(x_float, gain_vec):
    row_mean = lax.optimization_barrier(jnp.mean(x_float, axis=-1, keepdims=True))
    centered = x_float - row_mean
    inv_std = lax.rsqrt(lax.optimization_barrier(jnp.mean(centered * centered, axis=-1, keepdims=True)) + NORM_EPS)
    x_hat = centered * inv_std
    normed = (x_hat * gain_vec.astype(jnp.float32)).astype(jnp.bfloat16)
    return (x_hat, inv_std, normed)

def norm_backward(grad_out, x_hat, inv_std, gain_vec):
    grad_hat = grad_out * gain_vec.astype(jnp.float32)
    grad_gain = lax.optimization_barrier(jnp.sum(grad_out * x_hat, axis=0))
    inner_term = grad_hat - lax.optimization_barrier(jnp.mean(grad_hat, axis=-1, keepdims=True)) - x_hat * lax.optimization_barrier(jnp.mean(grad_hat * x_hat, axis=-1, keepdims=True))
    return (inv_std * inner_term, grad_gain)

def rope_tables(doc_len, span_len, head_width):
    doc_len = doc_len.astype(jnp.int32)
    doc_end = jnp.cumsum(doc_len).astype(jnp.int32)
    doc_start = doc_end - doc_len
    places = jnp.arange(span_len, dtype=jnp.int32)
    inside = places[:, None] >= doc_start[None, :]
    begins = lax.optimization_barrier(jnp.max(jnp.where(inside, doc_start[None, :], 0), axis=1)).astype(jnp.int32)
    segment = lax.optimization_barrier(jnp.sum((places[:, None] >= doc_end[None, :]).astype(jnp.int32), axis=1)).astype(jnp.int32)
    offset = (places - begins).astype(jnp.float32)
    half_width = head_width // 2
    frequency = ROPE_BASE ** (-(jnp.arange(half_width, dtype=jnp.float32) * (2.0 / head_width)))
    angles = offset[:, None] * frequency[None, :]
    angles = jnp.concatenate([angles, angles], axis=1)
    return (jnp.cos(angles), jnp.sin(angles), segment)

def rotate(values_in, cosines, sines):
    half_width = values_in.shape[-1] // 2
    turned = jnp.concatenate([-values_in[..., half_width:], values_in[..., :half_width]], axis=-1)
    return values_in * cosines[:, None, :] + turned * sines[:, None, :]

def rotate_back(grads_in, cosines, sines):
    half_width = grads_in.shape[-1] // 2
    scaled = grads_in * sines[:, None, :]
    turned = jnp.concatenate([scaled[..., half_width:], -scaled[..., :half_width]], axis=-1)
    return grads_in * cosines[:, None, :] + turned

def masked_scores(query_blk, keys_all, same_doc):
    score_scale = query_blk.shape[-1] ** (-0.5)
    scores = jnp.einsum('bhe,che->hbc', query_blk.astype(jnp.float32), keys_all.astype(jnp.float32)) * score_scale
    return jnp.where(same_doc[None, :, :], scores, MASK_FILL)

def attend_rows(query_blk, keys_all, vals_all, same_doc):
    scores = masked_scores(query_blk, keys_all, same_doc)
    row_max = lax.optimization_barrier(jnp.max(scores, axis=-1, keepdims=True))
    expo_vals = jnp.exp(scores - row_max)
    row_total = lax.optimization_barrier(jnp.sum(expo_vals, axis=-1, keepdims=True))
    prob_b = (expo_vals / row_total).astype(jnp.bfloat16)
    out_rows = jnp.einsum('hbc,che->bhe', prob_b.astype(jnp.float32), vals_all.astype(jnp.float32))
    log_total = (row_max + jnp.log(row_total))[:, :, 0]
    return (out_rows.astype(jnp.bfloat16), log_total)

def attend_rows_back(query_blk, out_blk, grad_blk, log_blk, keys_all, vals_all, same_doc):
    score_scale = query_blk.shape[-1] ** (-0.5)
    scores = masked_scores(query_blk, keys_all, same_doc)
    probs = jnp.exp(scores - log_blk[:, :, None])
    prob_b = probs.astype(jnp.bfloat16)
    grad_f = grad_blk.astype(jnp.float32)
    grad_vals = jnp.einsum('hbc,bhe->che', prob_b.astype(jnp.float32), grad_f)
    grad_prob = jnp.einsum('bhe,che->hbc', grad_f, vals_all.astype(jnp.float32))
    delta_row = lax.optimization_barrier(jnp.sum(grad_f * out_blk.astype(jnp.float32), axis=-1)).T
    grad_score = (probs * (grad_prob - delta_row[:, :, None]) * score_scale).astype(jnp.bfloat16)
    grad_query = jnp.einsum('hbc,che->bhe', grad_score.astype(jnp.float32), keys_all.astype(jnp.float32))
    grad_keys = jnp.einsum('hbc,bhe->che', grad_score.astype(jnp.float32), query_blk.astype(jnp.float32))
    return (grad_query, grad_keys, grad_vals)

def attention_forward(query_rot, keys_all, vals_all, segment):
    row_count, head_count, head_width = query_rot.shape
    block_rows = min(512, row_count)
    block_count = row_count // block_rows
    query_blocks = query_rot.reshape(block_count, block_rows, head_count, head_width)
    seg_blocks = segment.reshape(block_count, block_rows)

    def one_block(block_args):
        query_blk, seg_blk = block_args
        same_doc = seg_blk[:, None] == segment[None, :]
        return attend_rows(query_blk, keys_all, vals_all, same_doc)
    out_blocks, log_blocks = lax.map(one_block, (query_blocks, seg_blocks))
    return (out_blocks.reshape(row_count, head_count, head_width), log_blocks)

def attention_backward(query_rot, keys_all, vals_all, attn_heads, grad_heads, log_blocks, segment):
    row_count, head_count, head_width = query_rot.shape
    block_rows = min(512, row_count)
    block_count = row_count // block_rows
    shaped = (block_count, block_rows, head_count, head_width)

    def one_block(carry, block_args):
        keys_acc, vals_acc = carry
        query_blk, out_blk, grad_blk, log_blk, seg_blk = block_args
        same_doc = seg_blk[:, None] == segment[None, :]
        grad_query, grad_keys, grad_vals = attend_rows_back(query_blk, out_blk, grad_blk, log_blk, keys_all, vals_all, same_doc)
        return ((keys_acc + grad_keys, vals_acc + grad_vals), grad_query)
    zeros_acc = jnp.zeros((row_count, head_count, head_width), jnp.float32)
    (grad_keys, grad_vals), grad_query = lax.scan(one_block, (zeros_acc, zeros_acc), (query_rot.reshape(shaped), attn_heads.reshape(shaped), grad_heads.reshape(shaped), log_blocks, segment.reshape(block_count, block_rows)))
    return (grad_query.reshape(row_count, head_count, head_width), grad_keys, grad_vals)

def layer_pass(span_tok, span_docs, span_cot, gain_attn, w_qkv, w_attn_out, gain_mlp, w_in, w_mlp_out):
    f32 = jnp.float32
    bf16 = jnp.bfloat16
    span_len, width = span_tok.shape
    head_count = width // HD
    cosines, sines, segment = rope_tables(span_docs, span_len, HD)
    x_float = span_tok.astype(f32)
    hat_one, inv_one, normed_one = norm_forward(x_float, gain_attn)
    projected = jnp.stack([jnp.dot(normed_one, w_qkv[part_idx], preferred_element_type=f32) for part_idx in range(3)]).astype(bf16)
    split_heads = projected.reshape(3, span_len, head_count, HD)
    query_rot = rotate(split_heads[0].astype(f32), cosines, sines).astype(bf16)
    keys_all = rotate(split_heads[1].astype(f32), cosines, sines).astype(bf16)
    vals_all = split_heads[2]
    attn_heads, log_blocks = attention_forward(query_rot, keys_all, vals_all, segment)
    attn_flat = attn_heads.reshape(span_len, width)
    mixed_one = x_float + jnp.dot(attn_flat, w_attn_out, preferred_element_type=f32)
    hat_two, inv_two, normed_two = norm_forward(mixed_one, gain_mlp)
    act_in = jnp.dot(normed_two, w_in[0], preferred_element_type=f32)
    gate_in = jnp.dot(normed_two, w_in[1], preferred_element_type=f32)
    cdf_val = 0.5 * (1.0 + jax.scipy.special.erf(act_in * INV_ROOT_TWO))
    gelu_val = act_in * cdf_val
    hidden = (gelu_val * gate_in).astype(bf16)
    result = (mixed_one + jnp.dot(hidden, w_mlp_out, preferred_element_type=f32)).astype(bf16)
    cot_float = span_cot.astype(f32)
    grad_mlp_out = jnp.dot(hidden.T, span_cot, preferred_element_type=f32)
    grad_hidden = jnp.dot(span_cot, w_mlp_out.T, preferred_element_type=f32)
    gelu_slope = cdf_val + act_in * jnp.exp(-0.5 * act_in * act_in) * INV_ROOT_TWO_PI
    grad_act = (grad_hidden * gate_in * gelu_slope).astype(bf16)
    grad_gate = (grad_hidden * gelu_val).astype(bf16)
    grad_in = jnp.stack([jnp.dot(normed_two.T, grad_act, preferred_element_type=f32), jnp.dot(normed_two.T, grad_gate, preferred_element_type=f32)])
    grad_normed_two = jnp.dot(grad_act, w_in[0].T, preferred_element_type=f32) + jnp.dot(grad_gate, w_in[1].T, preferred_element_type=f32)
    back_two, grad_gain_mlp = norm_backward(grad_normed_two, hat_two, inv_two, gain_mlp)
    grad_mixed = cot_float + back_two
    grad_mixed_b = grad_mixed.astype(bf16)
    grad_attn_out = jnp.dot(attn_flat.T, grad_mixed_b, preferred_element_type=f32)
    grad_heads = jnp.dot(grad_mixed_b, w_attn_out.T, preferred_element_type=f32).astype(bf16).reshape(span_len, head_count, HD)
    grad_query, grad_keys, grad_vals = attention_backward(query_rot, keys_all, vals_all, attn_heads, grad_heads, log_blocks, segment)
    grad_query = rotate_back(grad_query, cosines, sines).astype(bf16)
    grad_keys = rotate_back(grad_keys, cosines, sines).astype(bf16)
    grad_proj = jnp.stack([grad_query, grad_keys, grad_vals.astype(bf16)]).reshape(3, span_len, width)
    grad_qkv = jnp.stack([jnp.dot(normed_one.T, grad_proj[part_idx], preferred_element_type=f32) for part_idx in range(3)])
    grad_normed_one = jnp.dot(grad_proj[0], w_qkv[0].T, preferred_element_type=f32)
    grad_normed_one = grad_normed_one + jnp.dot(grad_proj[1], w_qkv[1].T, preferred_element_type=f32)
    grad_normed_one = grad_normed_one + jnp.dot(grad_proj[2], w_qkv[2].T, preferred_element_type=f32)
    back_one, grad_gain_attn = norm_backward(grad_normed_one, hat_one, inv_one, gain_attn)
    grad_tok = grad_mixed + back_one
    return (result, grad_tok, grad_gain_attn, grad_qkv, grad_attn_out, grad_gain_mlp, grad_in, grad_mlp_out)

def reference(tokens, doc_lengths, gain_attn, w_qkv, w_attn_out, gain_mlp, w_in, w_mlp_out, cotangent):
    span_len = TOK_DEV * N_CTX
    width = tokens.shape[1]

    def span_step(carry, inputs):
        span_tok, span_docs, span_cot = inputs
        outcome = layer_pass(span_tok, span_docs, span_cot, gain_attn, w_qkv, w_attn_out, gain_mlp, w_in, w_mlp_out)
        summed = tuple((held + term for held, term in zip(carry, outcome[2:])))
        return (summed, (outcome[0], outcome[1]))
    start_sums = (jnp.zeros(gain_attn.shape, jnp.float32), jnp.zeros(w_qkv.shape, jnp.float32), jnp.zeros(w_attn_out.shape, jnp.float32), jnp.zeros(gain_mlp.shape, jnp.float32), jnp.zeros(w_in.shape, jnp.float32), jnp.zeros(w_mlp_out.shape, jnp.float32))
    span_count = doc_lengths.shape[0]
    sums, (results, grad_toks) = lax.scan(span_step, start_sums, (tokens.reshape(span_count, span_len, width), doc_lengths, cotangent.reshape(span_count, span_len, width)))
    return (results.reshape(-1, width), grad_toks.reshape(-1, width), sums[0], sums[1], sums[2], sums[3], sums[4], sums[5])
```

```python
import math

import jax
import jax.numpy as jnp
from jax import lax
from jax.sharding import PartitionSpec as P

HD = 64


NORM_EPS = 1e-05
ROPE_BASE = 160000.0
MASK_FILL = -1e30
INV_ROOT_TWO = 1.0 / math.sqrt(2.0)
INV_ROOT_TWO_PI = 1.0 / math.sqrt(2.0 * math.pi)


def norm_forward(x_float, gain_vec):
    row_mean = jnp.mean(x_float, axis=-1, keepdims=True)
    centered = x_float - row_mean
    inv_std = lax.rsqrt(jnp.mean(centered * centered, axis=-1, keepdims=True) + NORM_EPS)
    x_hat = centered * inv_std
    normed = (x_hat * gain_vec.astype(jnp.float32)).astype(jnp.bfloat16)
    return (x_hat, inv_std, normed)


def norm_backward(grad_out, x_hat, inv_std, gain_vec):
    grad_hat = grad_out * gain_vec.astype(jnp.float32)
    grad_gain = jnp.sum(grad_out * x_hat, axis=0)
    inner_term = (
        grad_hat
        - jnp.mean(grad_hat, axis=-1, keepdims=True)
        - x_hat * jnp.mean(grad_hat * x_hat, axis=-1, keepdims=True)
    )
    return (inv_std * inner_term, grad_gain)


def rope_tables(doc_len, span_len, head_width):
    doc_end = jnp.cumsum(doc_len)
    doc_start = doc_end - doc_len
    places = jnp.arange(span_len, dtype=jnp.int32)
    inside = places[:, None] >= doc_start[None, :]
    begins = jnp.max(jnp.where(inside, doc_start[None, :], 0), axis=1)
    segment = jnp.sum((places[:, None] >= doc_end[None, :]).astype(jnp.int32), axis=1)
    offset = (places - begins).astype(jnp.float32)
    half_width = head_width // 2
    frequency = ROPE_BASE ** (-(jnp.arange(half_width, dtype=jnp.float32) * (2.0 / head_width)))
    angles = offset[:, None] * frequency[None, :]
    angles = jnp.concatenate([angles, angles], axis=1)
    return (jnp.cos(angles), jnp.sin(angles), segment)


def rotate(values_in, cosines, sines):
    half_width = values_in.shape[-1] // 2
    turned = jnp.concatenate([-values_in[..., half_width:], values_in[..., :half_width]], axis=-1)
    return values_in * cosines[:, None, :] + turned * sines[:, None, :]


def rotate_back(grads_in, cosines, sines):
    half_width = grads_in.shape[-1] // 2
    scaled = grads_in * sines[:, None, :]
    turned = jnp.concatenate([scaled[..., half_width:], -scaled[..., :half_width]], axis=-1)
    return grads_in * cosines[:, None, :] + turned


def masked_scores(query_blk, keys_all, same_doc):
    score_scale = query_blk.shape[-1] ** (-0.5)
    scores = (
        jnp.einsum("bhe,che->hbc", query_blk, keys_all, preferred_element_type=jnp.float32)
        * score_scale
    )
    return jnp.where(same_doc[None, :, :], scores, MASK_FILL)


def attend_rows(query_blk, keys_all, vals_all, same_doc):
    scores = masked_scores(query_blk, keys_all, same_doc)
    row_max = jnp.max(scores, axis=-1, keepdims=True)
    expo_vals = jnp.exp(scores - row_max)
    row_total = jnp.sum(expo_vals, axis=-1, keepdims=True)
    prob_b = (expo_vals / row_total).astype(jnp.bfloat16)
    out_rows = jnp.einsum("hbc,che->bhe", prob_b, vals_all, preferred_element_type=jnp.float32)
    log_total = (row_max + jnp.log(row_total))[:, :, 0]
    return (out_rows.astype(jnp.bfloat16), log_total)


def attend_rows_back(query_blk, out_blk, grad_blk, log_blk, keys_all, vals_all, same_doc):
    score_scale = query_blk.shape[-1] ** (-0.5)
    scores = masked_scores(query_blk, keys_all, same_doc)
    probs = jnp.exp(scores - log_blk[:, :, None])
    prob_b = probs.astype(jnp.bfloat16)
    grad_vals = jnp.einsum("hbc,bhe->che", prob_b, grad_blk, preferred_element_type=jnp.float32)
    grad_prob = jnp.einsum("bhe,che->hbc", grad_blk, vals_all, preferred_element_type=jnp.float32)
    delta_row = jnp.sum(grad_blk.astype(jnp.float32) * out_blk.astype(jnp.float32), axis=-1).T
    grad_score = (probs * (grad_prob - delta_row[:, :, None]) * score_scale).astype(jnp.bfloat16)
    grad_query = jnp.einsum(
        "hbc,che->bhe", grad_score, keys_all, preferred_element_type=jnp.float32
    )
    grad_keys = jnp.einsum(
        "hbc,bhe->che", grad_score, query_blk, preferred_element_type=jnp.float32
    )
    return (grad_query, grad_keys, grad_vals)


BOTH = ("dp", "ctx")


def add_pair(part):
    part_b = part.astype(jnp.bfloat16)
    ways = lax.axis_size("tensor")
    total = part_b.astype(jnp.float32)
    for step in range(1, ways):
        pairs = [(src, (src + step) % ways) for src in range(ways)]
        total = total + lax.ppermute(part_b, "tensor", pairs).astype(jnp.float32)
    return total


def own_rows(block, axis):
    ways = lax.axis_size("ctx")
    rows = block.shape[axis] // ways
    return lax.dynamic_slice_in_dim(block, lax.axis_index("ctx") * rows, rows, axis)


def local(tokens, doc_lengths, gain_attn, w_qkv, w_attn_out, gain_mlp, w_in, w_mlp_out, cotangent):
    f32 = jnp.float32
    bf16 = jnp.bfloat16
    gains = lax.all_gather(jnp.stack([gain_attn, gain_mlp]), "dp", axis=1, tiled=True)
    gain_one, gain_two = gains[0], gains[1]
    w_query_all = lax.all_gather(own_rows(w_qkv, 1), BOTH, axis=1, tiled=True)
    w_out_all = lax.all_gather(own_rows(w_attn_out.T, 0), BOTH, axis=0, tiled=True)
    w_in_all = lax.all_gather(own_rows(w_in, 1), BOTH, axis=1, tiled=True)
    w_down_all = lax.all_gather(own_rows(w_mlp_out.T, 0), BOTH, axis=0, tiled=True)
    ctx_ways = lax.axis_size("ctx")
    tok_rows = tokens.shape[0]
    span_len = tok_rows * ctx_ways
    local_width = w_query_all.shape[2]
    per_group = local_width // ctx_ways
    heads_here = per_group // HD
    cosines, sines, segment = rope_tables(doc_lengths[0], span_len, HD)
    same_doc = segment[:, None] == segment[None, :]
    x_float = tokens.astype(f32)
    hat_one, inv_one, normed_one = norm_forward(x_float, gain_one)
    projected = jnp.einsum(
        "td,kde->kte", normed_one, w_query_all, preferred_element_type=f32
    ).astype(bf16)
    projected = projected.reshape(3, tok_rows, ctx_ways, per_group)
    spread = lax.all_to_all(projected, "ctx", split_axis=2, concat_axis=1, tiled=True)
    spread = spread.reshape(3, span_len, heads_here, HD)
    query_rot = rotate(spread[0].astype(f32), cosines, sines).astype(bf16)
    keys_all = rotate(spread[1].astype(f32), cosines, sines).astype(bf16)
    vals_all = spread[2]
    attn_heads, log_rows = attend_rows(query_rot, keys_all, vals_all, same_doc)
    returned = lax.all_to_all(
        attn_heads.reshape(span_len, 1, per_group), "ctx", split_axis=0, concat_axis=1, tiled=True
    )
    attn_flat = returned.reshape(tok_rows, local_width)
    attn_total = add_pair(
        jnp.einsum("te,de->td", attn_flat, w_out_all, preferred_element_type=f32)
    )
    mixed_one = x_float + attn_total
    hat_two, inv_two, normed_two = norm_forward(mixed_one, gain_two)
    pair_in = jnp.einsum("td,kde->kte", normed_two, w_in_all, preferred_element_type=f32)
    act_in = pair_in[0]
    gate_in = pair_in[1]
    cdf_val = 0.5 * (1.0 + jax.scipy.special.erf(act_in * INV_ROOT_TWO))
    gelu_val = act_in * cdf_val
    hidden = (gelu_val * gate_in).astype(bf16)
    mlp_total = add_pair(
        jnp.einsum("tf,df->td", hidden, w_down_all, preferred_element_type=f32)
    )
    result = (mixed_one + mlp_total).astype(bf16)
    cot_float = cotangent.astype(f32)
    grad_mlp_out = jnp.einsum("td,tf->df", cotangent, hidden, preferred_element_type=f32)
    share_down = lax.psum_scatter(
        grad_mlp_out.astype(bf16), BOTH, scatter_dimension=0, tiled=True
    )
    grad_hidden = jnp.einsum("td,df->tf", cotangent, w_down_all, preferred_element_type=f32)
    gelu_slope = cdf_val + act_in * jnp.exp(-0.5 * act_in * act_in) * INV_ROOT_TWO_PI
    grad_pair = jnp.stack(
        [(grad_hidden * gate_in * gelu_slope).astype(bf16), (grad_hidden * gelu_val).astype(bf16)]
    )
    grad_in = [
        jnp.einsum("td,te->de", normed_two, grad_pair[k], preferred_element_type=f32)
        for k in range(2)
    ]
    share_in = [
        lax.psum_scatter(grad_in[k].astype(bf16), BOTH, scatter_dimension=0, tiled=True)
        for k in range(2)
    ]
    grad_normed_two = add_pair(
        jnp.einsum("kte,kde->td", grad_pair, w_in_all, preferred_element_type=f32)
    )
    back_two, grad_gain_mlp = norm_backward(grad_normed_two, hat_two, inv_two, gain_two)
    grad_mixed = cot_float + back_two
    grad_mixed_b = grad_mixed.astype(bf16)
    grad_attn_out = jnp.einsum("td,te->de", grad_mixed_b, attn_flat, preferred_element_type=f32)
    share_out = lax.psum_scatter(
        grad_attn_out.astype(bf16), BOTH, scatter_dimension=0, tiled=True
    )
    grad_local = jnp.einsum(
        "td,de->te", grad_mixed_b, w_out_all, preferred_element_type=f32
    ).astype(bf16)
    grad_spread = lax.all_to_all(
        grad_local.reshape(tok_rows, ctx_ways, per_group),
        "ctx",
        split_axis=1,
        concat_axis=0,
        tiled=True,
    )
    grad_heads = grad_spread.reshape(span_len, heads_here, HD)
    grad_query, grad_keys, grad_vals = attend_rows_back(
        query_rot, attn_heads, grad_heads, log_rows, keys_all, vals_all, same_doc
    )
    grad_query = rotate_back(grad_query, cosines, sines).astype(bf16)
    grad_keys = rotate_back(grad_keys, cosines, sines).astype(bf16)
    grad_stack = jnp.stack([grad_query, grad_keys, grad_vals.astype(bf16)]).reshape(
        3, span_len, 1, per_group
    )
    grad_back = lax.all_to_all(grad_stack, "ctx", split_axis=1, concat_axis=2, tiled=True)
    grad_proj = grad_back.reshape(3, tok_rows, local_width)
    grad_qkv = [
        jnp.einsum("td,te->de", normed_one, grad_proj[k], preferred_element_type=f32)
        for k in range(3)
    ]
    share_qkv = lax.psum_scatter(
        jnp.concatenate(grad_qkv, axis=1).astype(bf16), BOTH, scatter_dimension=0, tiled=True
    )
    share_qkv = share_qkv.reshape(-1, 3, local_width).transpose(1, 0, 2)
    grad_normed_one = add_pair(
        jnp.einsum("kte,kde->td", grad_proj, w_query_all, preferred_element_type=f32)
    )
    back_one, grad_gain_attn = norm_backward(grad_normed_one, hat_one, inv_one, gain_one)
    grad_tok = grad_mixed + back_one
    gain_sums = lax.psum(jnp.stack([grad_gain_attn, grad_gain_mlp]), BOTH)
    gain_rows = gain_attn.shape[0]
    gain_own = lax.dynamic_slice_in_dim(
        gain_sums, lax.axis_index("dp") * gain_rows, gain_rows, 1
    )
    own_down = lax.all_gather(share_down, "ctx", axis=0, tiled=True).astype(f32).T
    own_in = lax.all_gather(jnp.stack(share_in), "ctx", axis=1, tiled=True).astype(f32)
    own_out = lax.all_gather(share_out, "ctx", axis=0, tiled=True).astype(f32).T
    own_qkv = lax.all_gather(share_qkv, "ctx", axis=1, tiled=True).astype(f32)
    return (result, grad_tok, gain_own[0], own_qkv, own_out, gain_own[1], own_in, own_down)


def solution(mesh):
    in_specs = (
        P(("dp", "ctx"), None),
        P("dp", None),
        P("dp"),
        P(None, "dp", "tensor"),
        P("tensor", "dp"),
        P("dp"),
        P(None, "dp", "tensor"),
        P("tensor", "dp"),
        P(("dp", "ctx"), None),
    )
    out_specs = (
        P(("dp", "ctx"), None),
        P(("dp", "ctx"), None),
        P("dp"),
        P(None, "dp", "tensor"),
        P("tensor", "dp"),
        P("dp"),
        P(None, "dp", "tensor"),
        P("tensor", "dp"),
    )
    return jax.shard_map(local, mesh=mesh, in_specs=in_specs, out_specs=out_specs, check_vma=False)
```

```python
import math

import jax
import jax.numpy as jnp
from jax import lax
from jax.sharding import PartitionSpec as P

HD = 64


NORM_EPS = 1e-05
ROPE_BASE = 160000.0
MASK_FILL = -1e30
INV_ROOT_TWO = 1.0 / math.sqrt(2.0)
INV_ROOT_TWO_PI = 1.0 / math.sqrt(2.0 * math.pi)


def norm_forward(x_float, gain_vec):
    row_mean = jnp.mean(x_float, axis=-1, keepdims=True)
    centered = x_float - row_mean
    inv_std = lax.rsqrt(jnp.mean(centered * centered, axis=-1, keepdims=True) + NORM_EPS)
    x_hat = centered * inv_std
    normed = (x_hat * gain_vec.astype(jnp.float32)).astype(jnp.bfloat16)
    return (x_hat, inv_std, normed)


def norm_backward(grad_out, x_hat, inv_std, gain_vec):
    grad_hat = grad_out * gain_vec.astype(jnp.float32)
    grad_gain = jnp.sum(grad_out * x_hat, axis=0)
    inner_term = (
        grad_hat
        - jnp.mean(grad_hat, axis=-1, keepdims=True)
        - x_hat * jnp.mean(grad_hat * x_hat, axis=-1, keepdims=True)
    )
    return (inv_std * inner_term, grad_gain)


def rope_tables(doc_len, span_len, head_width):
    doc_end = jnp.cumsum(doc_len)
    doc_start = doc_end - doc_len
    places = jnp.arange(span_len, dtype=jnp.int32)
    inside = places[:, None] >= doc_start[None, :]
    begins = jnp.max(jnp.where(inside, doc_start[None, :], 0), axis=1)
    segment = jnp.sum((places[:, None] >= doc_end[None, :]).astype(jnp.int32), axis=1)
    offset = (places - begins).astype(jnp.float32)
    half_width = head_width // 2
    frequency = ROPE_BASE ** (-(jnp.arange(half_width, dtype=jnp.float32) * (2.0 / head_width)))
    angles = offset[:, None] * frequency[None, :]
    angles = jnp.concatenate([angles, angles], axis=1)
    return (jnp.cos(angles), jnp.sin(angles), segment)


def rotate(values_in, cosines, sines):
    half_width = values_in.shape[-1] // 2
    turned = jnp.concatenate([-values_in[..., half_width:], values_in[..., :half_width]], axis=-1)
    return values_in * cosines[:, None, :] + turned * sines[:, None, :]


def rotate_back(grads_in, cosines, sines):
    half_width = grads_in.shape[-1] // 2
    scaled = grads_in * sines[:, None, :]
    turned = jnp.concatenate([scaled[..., half_width:], -scaled[..., :half_width]], axis=-1)
    return grads_in * cosines[:, None, :] + turned


def masked_scores(query_blk, keys_all, same_doc):
    score_scale = query_blk.shape[-1] ** (-0.5)
    scores = (
        jnp.einsum("bhe,che->hbc", query_blk, keys_all, preferred_element_type=jnp.float32)
        * score_scale
    )
    return jnp.where(same_doc[None, :, :], scores, MASK_FILL)


def attend_rows(query_blk, keys_all, vals_all, same_doc):
    scores = masked_scores(query_blk, keys_all, same_doc)
    row_max = jnp.max(scores, axis=-1, keepdims=True)
    expo_vals = jnp.exp(scores - row_max)
    row_total = jnp.sum(expo_vals, axis=-1, keepdims=True)
    prob_b = (expo_vals / row_total).astype(jnp.bfloat16)
    out_rows = jnp.einsum("hbc,che->bhe", prob_b, vals_all, preferred_element_type=jnp.float32)
    log_total = (row_max + jnp.log(row_total))[:, :, 0]
    return (out_rows.astype(jnp.bfloat16), log_total)


def attend_rows_back(query_blk, out_blk, grad_blk, log_blk, keys_all, vals_all, same_doc):
    score_scale = query_blk.shape[-1] ** (-0.5)
    scores = masked_scores(query_blk, keys_all, same_doc)
    probs = jnp.exp(scores - log_blk[:, :, None])
    prob_b = probs.astype(jnp.bfloat16)
    grad_vals = jnp.einsum("hbc,bhe->che", prob_b, grad_blk, preferred_element_type=jnp.float32)
    grad_prob = jnp.einsum("bhe,che->hbc", grad_blk, vals_all, preferred_element_type=jnp.float32)
    delta_row = jnp.sum(grad_blk.astype(jnp.float32) * out_blk.astype(jnp.float32), axis=-1).T
    grad_score = (probs * (grad_prob - delta_row[:, :, None]) * score_scale).astype(jnp.bfloat16)
    grad_query = jnp.einsum(
        "hbc,che->bhe", grad_score, keys_all, preferred_element_type=jnp.float32
    )
    grad_keys = jnp.einsum(
        "hbc,bhe->che", grad_score, query_blk, preferred_element_type=jnp.float32
    )
    return (grad_query, grad_keys, grad_vals)


BOTH = ("dp", "ctx")
LANES = 128


def add_pair(part):
    part_b = part.astype(jnp.bfloat16)
    ways = lax.axis_size("tensor")
    total = part_b.astype(jnp.float32)
    for step in range(1, ways):
        pairs = [(src, (src + step) % ways) for src in range(ways)]
        total = total + lax.ppermute(part_b, "tensor", pairs).astype(jnp.float32)
    return total


def own_rows(block, axis):
    ways = lax.axis_size("ctx")
    rows = block.shape[axis] // ways
    return lax.dynamic_slice_in_dim(block, lax.axis_index("ctx") * rows, rows, axis)


def local(tokens, doc_lengths, gain_attn, w_qkv, w_attn_out, gain_mlp, w_in, w_mlp_out, cotangent):
    f32 = jnp.float32
    bf16 = jnp.bfloat16
    units = w_in.shape[2]
    padded = -(-units // LANES) * LANES
    local_width = w_qkv.shape[2]
    gain_cols = jnp.pad(jnp.stack([gain_attn, gain_mlp], axis=1), ((0, 0), (0, LANES - 2)))
    attn_block = own_rows(
        jnp.concatenate([w_qkv[0], w_qkv[1], w_qkv[2], w_attn_out.T, gain_cols], axis=1), 0
    )
    attn_all = lax.all_gather(attn_block, BOTH, axis=0, tiled=True)
    mlp_parts = jnp.stack([own_rows(w_in[0], 0), own_rows(w_in[1], 0), own_rows(w_mlp_out.T, 0)])
    mlp_parts = jnp.pad(mlp_parts, ((0, 0), (0, 0), (0, padded - units)))
    mlp_block = jnp.concatenate([mlp_parts[0], mlp_parts[1], mlp_parts[2]], axis=1)
    mlp_block, attn_all = lax.optimization_barrier((mlp_block, attn_all))
    mlp_all = lax.all_gather(mlp_block, BOTH, axis=0, tiled=True)
    qkv_width = 3 * local_width
    w_query_all = attn_all[:, :qkv_width]
    w_out_all = attn_all[:, qkv_width : qkv_width + local_width]
    gain_one = attn_all[:, qkv_width + local_width]
    gain_two = attn_all[:, qkv_width + local_width + 1]
    w_in_all = mlp_all[:, : 2 * padded]
    w_down_all = mlp_all[:, 2 * padded :]
    ctx_ways = lax.axis_size("ctx")
    tok_rows = tokens.shape[0]
    span_len = tok_rows * ctx_ways
    per_group = local_width // ctx_ways
    heads_here = per_group // HD
    cosines, sines, segment = rope_tables(doc_lengths[0], span_len, HD)
    same_doc = segment[:, None] == segment[None, :]
    x_float = tokens.astype(f32)
    hat_one, inv_one, normed_one = norm_forward(x_float, gain_one)
    projected = jnp.dot(normed_one, w_query_all, preferred_element_type=f32).astype(bf16)
    projected = jnp.stack(jnp.split(projected, 3, axis=1))
    projected = projected.reshape(3, tok_rows, ctx_ways, per_group)
    spread = lax.all_to_all(projected, "ctx", split_axis=2, concat_axis=1, tiled=True)
    spread = spread.reshape(3, span_len, heads_here, HD)
    query_rot = rotate(spread[0].astype(f32), cosines, sines).astype(bf16)
    keys_all = rotate(spread[1].astype(f32), cosines, sines).astype(bf16)
    vals_all = spread[2]
    attn_heads, log_rows = attend_rows(query_rot, keys_all, vals_all, same_doc)
    returned = lax.all_to_all(
        attn_heads.reshape(span_len, 1, per_group), "ctx", split_axis=0, concat_axis=1, tiled=True
    )
    attn_flat = returned.reshape(tok_rows, local_width)
    attn_total = add_pair(
        jnp.einsum("te,de->td", attn_flat, w_out_all, preferred_element_type=f32)
    )
    mixed_one = x_float + attn_total
    hat_two, inv_two, normed_two = norm_forward(mixed_one, gain_two)
    pair_in = jnp.dot(normed_two, w_in_all, preferred_element_type=f32)
    act_in = pair_in[:, :padded]
    gate_in = pair_in[:, padded:]
    cdf_val = 0.5 * (1.0 + jax.scipy.special.erf(act_in * INV_ROOT_TWO))
    gelu_val = act_in * cdf_val
    hidden = (gelu_val * gate_in).astype(bf16)
    mlp_total = add_pair(
        jnp.einsum("tf,df->td", hidden, w_down_all, preferred_element_type=f32)
    )
    result = (mixed_one + mlp_total).astype(bf16)
    cot_float = cotangent.astype(f32)
    grad_mlp_out = jnp.einsum("td,tf->df", cotangent, hidden, preferred_element_type=f32)
    grad_hidden = jnp.einsum("td,df->tf", cotangent, w_down_all, preferred_element_type=f32)
    gelu_slope = cdf_val + act_in * jnp.exp(-0.5 * act_in * act_in) * INV_ROOT_TWO_PI
    grad_pair = jnp.concatenate(
        [(grad_hidden * gate_in * gelu_slope).astype(bf16), (grad_hidden * gelu_val).astype(bf16)],
        axis=1,
    )
    grad_in = jnp.einsum("td,te->de", normed_two, grad_pair, preferred_element_type=f32)
    share_mlp = lax.psum_scatter(
        jnp.concatenate([grad_in.astype(bf16), grad_mlp_out.astype(bf16)], axis=1),
        BOTH,
        scatter_dimension=0,
        tiled=True,
    )
    grad_normed_two = add_pair(
        jnp.einsum("te,de->td", grad_pair, w_in_all, preferred_element_type=f32)
    )
    back_two, grad_gain_mlp = norm_backward(grad_normed_two, hat_two, inv_two, gain_two)
    grad_mixed = cot_float + back_two
    grad_mixed_b = grad_mixed.astype(bf16)
    grad_attn_out = jnp.einsum("td,te->de", grad_mixed_b, attn_flat, preferred_element_type=f32)
    grad_local = jnp.einsum(
        "td,de->te", grad_mixed_b, w_out_all, preferred_element_type=f32
    ).astype(bf16)
    grad_spread = lax.all_to_all(
        grad_local.reshape(tok_rows, ctx_ways, per_group),
        "ctx",
        split_axis=1,
        concat_axis=0,
        tiled=True,
    )
    grad_heads = grad_spread.reshape(span_len, heads_here, HD)
    grad_query, grad_keys, grad_vals = attend_rows_back(
        query_rot, attn_heads, grad_heads, log_rows, keys_all, vals_all, same_doc
    )
    grad_query = rotate_back(grad_query, cosines, sines).astype(bf16)
    grad_keys = rotate_back(grad_keys, cosines, sines).astype(bf16)
    grad_stack = jnp.stack([grad_query, grad_keys, grad_vals.astype(bf16)]).reshape(
        3, span_len, 1, per_group
    )
    grad_back = lax.all_to_all(grad_stack, "ctx", split_axis=1, concat_axis=2, tiled=True)
    grad_proj = grad_back.reshape(3, tok_rows, local_width)
    grad_proj = jnp.concatenate([grad_proj[0], grad_proj[1], grad_proj[2]], axis=1)
    grad_qkv = jnp.einsum("td,te->de", normed_one, grad_proj, preferred_element_type=f32)
    grad_normed_one = add_pair(
        jnp.einsum("te,de->td", grad_proj, w_query_all, preferred_element_type=f32)
    )
    back_one, grad_gain_attn = norm_backward(grad_normed_one, hat_one, inv_one, gain_one)
    grad_tok = grad_mixed + back_one
    gain_grads = jnp.pad(
        jnp.stack([grad_gain_attn, grad_gain_mlp], axis=1), ((0, 0), (0, LANES - 2))
    )
    share_attn = lax.psum_scatter(
        jnp.concatenate(
            [grad_qkv.astype(bf16), grad_attn_out.astype(bf16), gain_grads.astype(bf16)], axis=1
        ),
        BOTH,
        scatter_dimension=0,
        tiled=True,
    )
    own_mlp = lax.all_gather(share_mlp, "ctx", axis=0, tiled=True)
    own_attn = lax.all_gather(share_attn, "ctx", axis=0, tiled=True)
    own_in = jnp.stack([own_mlp[:, :units], own_mlp[:, padded : padded + units]]).astype(f32)
    own_down = own_mlp[:, 2 * padded : 2 * padded + units].astype(f32).T
    own_qkv = jnp.stack(jnp.split(own_attn[:, :qkv_width], 3, axis=1)).astype(f32)
    own_out = own_attn[:, qkv_width : qkv_width + local_width].astype(f32).T
    gain_own = own_attn[:, qkv_width + local_width : qkv_width + local_width + 2].astype(f32).T
    return (result, grad_tok, gain_own[0], own_qkv, own_out, gain_own[1], own_in, own_down)


def solution(mesh):
    in_specs = (
        P(("dp", "ctx"), None),
        P("dp", None),
        P("dp"),
        P(None, "dp", "tensor"),
        P("tensor", "dp"),
        P("dp"),
        P(None, "dp", "tensor"),
        P("tensor", "dp"),
        P(("dp", "ctx"), None),
    )
    out_specs = (
        P(("dp", "ctx"), None),
        P(("dp", "ctx"), None),
        P("dp"),
        P(None, "dp", "tensor"),
        P("tensor", "dp"),
        P("dp"),
        P(None, "dp", "tensor"),
        P("tensor", "dp"),
    )
    return jax.shard_map(local, mesh=mesh, in_specs=in_specs, out_specs=out_specs, check_vma=False)
```

```python
import math

import jax
import jax.numpy as jnp
from jax import lax
from jax.sharding import PartitionSpec as P

HD = 64


NORM_EPS = 1e-05
ROPE_BASE = 160000.0
MASK_FILL = -1e30
INV_ROOT_TWO = 1.0 / math.sqrt(2.0)
INV_ROOT_TWO_PI = 1.0 / math.sqrt(2.0 * math.pi)


def norm_forward(x_float, gain_vec):
    row_mean = jnp.mean(x_float, axis=-1, keepdims=True)
    centered = x_float - row_mean
    inv_std = lax.rsqrt(jnp.mean(centered * centered, axis=-1, keepdims=True) + NORM_EPS)
    x_hat = centered * inv_std
    normed = (x_hat * gain_vec.astype(jnp.float32)).astype(jnp.bfloat16)
    return (x_hat, inv_std, normed)


def norm_backward(grad_out, x_hat, inv_std, gain_vec):
    grad_hat = grad_out * gain_vec.astype(jnp.float32)
    grad_gain = jnp.sum(grad_out * x_hat, axis=0)
    inner_term = (
        grad_hat
        - jnp.mean(grad_hat, axis=-1, keepdims=True)
        - x_hat * jnp.mean(grad_hat * x_hat, axis=-1, keepdims=True)
    )
    return (inv_std * inner_term, grad_gain)


def rope_tables(doc_len, span_len, head_width):
    doc_end = jnp.cumsum(doc_len)
    doc_start = doc_end - doc_len
    places = jnp.arange(span_len, dtype=jnp.int32)
    inside = places[:, None] >= doc_start[None, :]
    begins = jnp.max(jnp.where(inside, doc_start[None, :], 0), axis=1)
    segment = jnp.sum((places[:, None] >= doc_end[None, :]).astype(jnp.int32), axis=1)
    offset = (places - begins).astype(jnp.float32)
    half_width = head_width // 2
    frequency = ROPE_BASE ** (-(jnp.arange(half_width, dtype=jnp.float32) * (2.0 / head_width)))
    angles = offset[:, None] * frequency[None, :]
    angles = jnp.concatenate([angles, angles], axis=1)
    return (jnp.cos(angles), jnp.sin(angles), segment)


def rotate(values_in, cosines, sines):
    half_width = values_in.shape[-1] // 2
    turned = jnp.concatenate([-values_in[..., half_width:], values_in[..., :half_width]], axis=-1)
    return values_in * cosines[:, None, :] + turned * sines[:, None, :]


def rotate_back(grads_in, cosines, sines):
    half_width = grads_in.shape[-1] // 2
    scaled = grads_in * sines[:, None, :]
    turned = jnp.concatenate([scaled[..., half_width:], -scaled[..., :half_width]], axis=-1)
    return grads_in * cosines[:, None, :] + turned


def masked_scores(query_blk, keys_all, same_doc):
    score_scale = query_blk.shape[-1] ** (-0.5)
    scores = (
        jnp.einsum("bhe,che->hbc", query_blk, keys_all, preferred_element_type=jnp.float32)
        * score_scale
    )
    return jnp.where(same_doc[None, :, :], scores, MASK_FILL)


def attend_rows(query_blk, keys_all, vals_all, same_doc):
    scores = masked_scores(query_blk, keys_all, same_doc)
    row_max = jnp.max(scores, axis=-1, keepdims=True)
    expo_vals = jnp.exp(scores - row_max)
    row_total = jnp.sum(expo_vals, axis=-1, keepdims=True)
    prob_b = (expo_vals / row_total).astype(jnp.bfloat16)
    out_rows = jnp.einsum("hbc,che->bhe", prob_b, vals_all, preferred_element_type=jnp.float32)
    log_total = (row_max + jnp.log(row_total))[:, :, 0]
    return (out_rows.astype(jnp.bfloat16), log_total)


def attend_rows_back(query_blk, out_blk, grad_blk, log_blk, keys_all, vals_all, same_doc):
    score_scale = query_blk.shape[-1] ** (-0.5)
    scores = masked_scores(query_blk, keys_all, same_doc)
    probs = jnp.exp(scores - log_blk[:, :, None])
    prob_b = probs.astype(jnp.bfloat16)
    grad_vals = jnp.einsum("hbc,bhe->che", prob_b, grad_blk, preferred_element_type=jnp.float32)
    grad_prob = jnp.einsum("bhe,che->hbc", grad_blk, vals_all, preferred_element_type=jnp.float32)
    delta_row = jnp.sum(grad_blk.astype(jnp.float32) * out_blk.astype(jnp.float32), axis=-1).T
    grad_score = (probs * (grad_prob - delta_row[:, :, None]) * score_scale).astype(jnp.bfloat16)
    grad_query = jnp.einsum(
        "hbc,che->bhe", grad_score, keys_all, preferred_element_type=jnp.float32
    )
    grad_keys = jnp.einsum(
        "hbc,bhe->che", grad_score, query_blk, preferred_element_type=jnp.float32
    )
    return (grad_query, grad_keys, grad_vals)


BOTH = ("dp", "ctx")
LANES = 128


def add_pair(part):
    part_b = part.astype(jnp.bfloat16)
    ways = lax.axis_size("tensor")
    total = part_b.astype(jnp.float32)
    for step in range(1, ways):
        pairs = [(src, (src + step) % ways) for src in range(ways)]
        total = total + lax.ppermute(part_b, "tensor", pairs).astype(jnp.float32)
    return total


def own_rows(block, axis):
    ways = lax.axis_size("ctx")
    rows = block.shape[axis] // ways
    return lax.dynamic_slice_in_dim(block, lax.axis_index("ctx") * rows, rows, axis)


def local(tokens, doc_lengths, gain_attn, w_qkv, w_attn_out, gain_mlp, w_in, w_mlp_out, cotangent):
    f32 = jnp.float32
    bf16 = jnp.bfloat16
    units = w_in.shape[2]
    padded = -(-units // LANES) * LANES
    local_width = w_qkv.shape[2]
    gain_cols = jnp.pad(jnp.stack([gain_attn, gain_mlp], axis=1), ((0, 0), (0, LANES - 2)))
    attn_block = own_rows(
        jnp.concatenate([w_qkv[0], w_qkv[1], w_qkv[2], w_attn_out.T, gain_cols], axis=1), 0
    )
    attn_all = lax.all_gather(attn_block, BOTH, axis=0, tiled=True)
    mlp_parts = jnp.stack([own_rows(w_in[0], 0), own_rows(w_in[1], 0), own_rows(w_mlp_out.T, 0)])
    mlp_parts = jnp.pad(mlp_parts, ((0, 0), (0, 0), (0, padded - units)))
    mlp_block = jnp.concatenate([mlp_parts[0], mlp_parts[1], mlp_parts[2]], axis=1)
    mlp_block, attn_all = lax.optimization_barrier((mlp_block, attn_all))
    mlp_all = lax.all_gather(mlp_block, BOTH, axis=0, tiled=True)
    qkv_width = 3 * local_width
    w_query_all = attn_all[:, :qkv_width]
    w_out_all = attn_all[:, qkv_width : qkv_width + local_width]
    gain_one = attn_all[:, qkv_width + local_width]
    gain_two = attn_all[:, qkv_width + local_width + 1]
    w_in_all = mlp_all[:, : 2 * padded]
    w_down_all = mlp_all[:, 2 * padded :]
    ctx_ways = lax.axis_size("ctx")
    tok_rows = tokens.shape[0]
    span_len = tok_rows * ctx_ways
    per_group = local_width // ctx_ways
    heads_here = per_group // HD
    cosines, sines, segment = rope_tables(doc_lengths[0], span_len, HD)
    same_doc = segment[:, None] == segment[None, :]
    x_float = tokens.astype(f32)
    hat_one, inv_one, normed_one = norm_forward(x_float, gain_one)
    projected = jnp.dot(normed_one, w_query_all, preferred_element_type=f32).astype(bf16)
    projected = jnp.stack(jnp.split(projected, 3, axis=1))
    projected = projected.reshape(3, tok_rows, ctx_ways, per_group)
    spread = lax.all_to_all(projected, "ctx", split_axis=2, concat_axis=1, tiled=True)
    spread = spread.reshape(3, span_len, heads_here, HD)
    query_rot = rotate(spread[0].astype(f32), cosines, sines).astype(bf16)
    keys_all = rotate(spread[1].astype(f32), cosines, sines).astype(bf16)
    vals_all = spread[2]
    attn_heads, log_rows = attend_rows(query_rot, keys_all, vals_all, same_doc)
    returned = lax.all_to_all(
        attn_heads.reshape(span_len, 1, per_group), "ctx", split_axis=0, concat_axis=1, tiled=True
    )
    attn_flat = returned.reshape(tok_rows, local_width)
    attn_total = add_pair(
        jnp.einsum("te,de->td", attn_flat, w_out_all, preferred_element_type=f32)
    )
    mixed_one = x_float + attn_total
    hat_two, inv_two, normed_two = norm_forward(mixed_one, gain_two)
    pair_in = jnp.dot(normed_two, w_in_all, preferred_element_type=f32)
    act_in = pair_in[:, :padded]
    gate_in = pair_in[:, padded:]
    cdf_val = 0.5 * (1.0 + jax.scipy.special.erf(act_in * INV_ROOT_TWO))
    gelu_val = act_in * cdf_val
    hidden = (gelu_val * gate_in).astype(bf16)
    mlp_total = add_pair(
        jnp.einsum("tf,df->td", hidden, w_down_all, preferred_element_type=f32)
    )
    result = (mixed_one + mlp_total).astype(bf16)
    cot_float = cotangent.astype(f32)
    grad_mlp_out = jnp.einsum("td,tf->df", cotangent, hidden, preferred_element_type=f32)
    grad_hidden = jnp.einsum("td,df->tf", cotangent, w_down_all, preferred_element_type=f32)
    gelu_slope = cdf_val + act_in * jnp.exp(-0.5 * act_in * act_in) * INV_ROOT_TWO_PI
    grad_pair = jnp.concatenate(
        [(grad_hidden * gate_in * gelu_slope).astype(bf16), (grad_hidden * gelu_val).astype(bf16)],
        axis=1,
    )
    grad_in = jnp.einsum("td,te->de", normed_two, grad_pair, preferred_element_type=f32)
    share_mlp = lax.psum_scatter(
        jnp.concatenate([grad_in.astype(bf16), grad_mlp_out.astype(bf16)], axis=1),
        BOTH,
        scatter_dimension=0,
        tiled=True,
    )
    grad_normed_two = add_pair(
        jnp.einsum("te,de->td", grad_pair, w_in_all, preferred_element_type=f32)
    )
    back_two, grad_gain_mlp = norm_backward(grad_normed_two, hat_two, inv_two, gain_two)
    grad_mixed = cot_float + back_two
    grad_mixed_b = grad_mixed.astype(bf16)
    grad_attn_out = jnp.einsum("td,te->de", grad_mixed_b, attn_flat, preferred_element_type=f32)
    grad_local = jnp.einsum(
        "td,de->te", grad_mixed_b, w_out_all, preferred_element_type=f32
    ).astype(bf16)
    grad_spread = lax.all_to_all(
        grad_local.reshape(tok_rows, ctx_ways, per_group),
        "ctx",
        split_axis=1,
        concat_axis=0,
        tiled=True,
    )
    grad_heads = grad_spread.reshape(span_len, heads_here, HD)
    grad_query, grad_keys, grad_vals = attend_rows_back(
        query_rot, attn_heads, grad_heads, log_rows, keys_all, vals_all, same_doc
    )
    grad_query = rotate_back(grad_query, cosines, sines).astype(bf16)
    grad_keys = rotate_back(grad_keys, cosines, sines).astype(bf16)
    grad_stack = jnp.stack([grad_query, grad_keys, grad_vals.astype(bf16)]).reshape(
        3, span_len, 1, per_group
    )
    grad_back = lax.all_to_all(grad_stack, "ctx", split_axis=1, concat_axis=2, tiled=True)
    grad_proj = grad_back.reshape(3, tok_rows, local_width)
    grad_proj = jnp.concatenate([grad_proj[0], grad_proj[1], grad_proj[2]], axis=1)
    grad_qkv = jnp.einsum("td,te->de", normed_one, grad_proj, preferred_element_type=f32)
    grad_normed_one = add_pair(
        jnp.einsum("te,de->td", grad_proj, w_query_all, preferred_element_type=f32)
    )
    back_one, grad_gain_attn = norm_backward(grad_normed_one, hat_one, inv_one, gain_one)
    grad_tok = grad_mixed + back_one
    gain_grads = jnp.pad(
        jnp.stack([grad_gain_attn, grad_gain_mlp], axis=1), ((0, 0), (0, LANES - 2))
    )
    attn_grads = jnp.concatenate(
        [grad_qkv.astype(bf16), grad_attn_out.astype(bf16), gain_grads.astype(bf16)], axis=1
    )
    attn_grads, share_mlp = lax.optimization_barrier((attn_grads, share_mlp))
    share_attn = lax.psum_scatter(attn_grads, BOTH, scatter_dimension=0, tiled=True)
    own_mlp = lax.all_gather(share_mlp, "ctx", axis=0, tiled=True)
    own_attn = lax.all_gather(share_attn, "ctx", axis=0, tiled=True)
    own_in = jnp.stack([own_mlp[:, :units], own_mlp[:, padded : padded + units]]).astype(f32)
    own_down = own_mlp[:, 2 * padded : 2 * padded + units].astype(f32).T
    own_qkv = jnp.stack(jnp.split(own_attn[:, :qkv_width], 3, axis=1)).astype(f32)
    own_out = own_attn[:, qkv_width : qkv_width + local_width].astype(f32).T
    gain_own = own_attn[:, qkv_width + local_width : qkv_width + local_width + 2].astype(f32).T
    return (result, grad_tok, gain_own[0], own_qkv, own_out, gain_own[1], own_in, own_down)


def solution(mesh):
    in_specs = (
        P(("dp", "ctx"), None),
        P("dp", None),
        P("dp"),
        P(None, "dp", "tensor"),
        P("tensor", "dp"),
        P("dp"),
        P(None, "dp", "tensor"),
        P("tensor", "dp"),
        P(("dp", "ctx"), None),
    )
    out_specs = (
        P(("dp", "ctx"), None),
        P(("dp", "ctx"), None),
        P("dp"),
        P(None, "dp", "tensor"),
        P("tensor", "dp"),
        P("dp"),
        P(None, "dp", "tensor"),
        P("tensor", "dp"),
    )
    return jax.shard_map(local, mesh=mesh, in_specs=in_specs, out_specs=out_specs, check_vma=False)
```
